32 devices in a mesh: row: 4 (over y, core), col: 8 (over z, x).
Axes of the slice: x: 2, y: 2, z: 4, core: 2. Of those that a mesh axis runs over, the one named last changes fastest.
Arguments:
- near_blocks: bfloat16 [64, 16, 512, 512], P(('row', 'col')), may hold values from -2 to 9, as said below
- leaf_basis: bfloat16 [64, 512, 512], P(('row', 'col')), may hold values from -1 to 2, as said below
- near_cols: int32 [64, 16], P(('row', 'col')), may hold values from 0 to 63, as said below
- near_count: int32 [64], P(('row', 'col')), may hold values from 1 to 16, as said below
- children: int32 [32, 2], replicated, may hold values from 0 to 63, as said below
- parent_basis: bfloat16 [32, 256, 256], P(('row', 'col')), may hold values from -1 to 2, as said below
- far_coupling: float32 [32, 128, 128], P(('row', 'col')), may hold values from -0.25 to 0.25
Outputs:
- leaf_factor: float32 [64, 384, 384], P(('row', 'col'))
- near_schur: float32 [64, 16, 128, 128], P(('row', 'col'))
- top_factor: float32 [32, 128, 128], P(('row', 'col'))
- top_schur: float32 [32, 128, 128], P(('row', 'col'))
The draws below stay inside these ranges and needn't reach their ends.
Inputs may be any that keep to these rules, and one draw needn't show every extreme that they name: near_cols[i, 0] = i; for 1 <= t < near_count[i] the entries near_cols[i, t] are distinct leaves other than i of i's group, the leaves 16 * g to 16 * g + 15 with g = i // 16; slots t >= near_count[i] hold i. `near_count`: some leaf has 16 live slots. Parent p belongs to group g = 2 * p // 16; children[p, 0] is a leaf of group g and children[p, 1] a leaf of group g + 1 - 2 * (g % 2); every leaf is a child of exactly one parent. near_blocks[i, 0] is symmetric positive definite. `leaf_basis`: each basis is nonsingular. `parent_basis`: each basis is nonsingular.
All inputs are finite; a program needn't handle non-finite values.
Results may differ from the reference program's by a relative error of at most 0.0015.
Values may be sent and summed in bfloat16 or wider, within the bound.
A program may use at most 192 MiB of HBM per device.

```python
import jax
import jax.numpy as jnp
from jax import lax

LEAF = 512
RANK = 128
NB = 16
GROUP = 16
LEAVES = 64
PARENTS = 32


def draw_near_blocks(key, part):
    key_noise = jax.random.fold_in(key, 101)
    key_diag = jax.random.fold_in(key, 102)
    shape = (LEAVES, NB, LEAF, LEAF)
    noise = jnp.clip(jax.random.normal(key_noise, shape, jnp.float32), -5.0, 5.0)
    diag_values = jnp.exp(jax.random.uniform(key_diag, (LEAVES, LEAF), jnp.float32, 1.3863, 2.0794))
    self_noise = noise[:, 0]
    sym_scale = 1.25 / (LEAF ** 0.5 * 1.41421356)
    symmetric = (self_noise + jnp.swapaxes(self_noise, 1, 2)) * sym_scale
    identity = jnp.eye(LEAF, dtype=jnp.float32)
    self_block = symmetric + identity[None] * diag_values[:, None, :] + 0.04
    others = noise[:, 1:] * 0.1
    blocks = jnp.concatenate([self_block[:, None], others], axis=1)
    return blocks.astype(jnp.bfloat16)


def near_identity(key, count, order):
    shape = (count, order, order)
    noise = jnp.clip(jax.random.normal(key, shape, jnp.float32), -5.0, 5.0)
    identity = jnp.eye(order, dtype=jnp.float32)
    return (identity[None] + noise * (0.2 / order ** 0.5)).astype(jnp.bfloat16)


def draw_leaf_basis(key, part):
    return near_identity(jax.random.fold_in(key, 201), LEAVES, LEAF)


def draw_parent_basis(key, part):
    return near_identity(jax.random.fold_in(key, 202), PARENTS, 2 * RANK)


def count_draw(key):
    key_counts = jax.random.fold_in(key, 7)
    key_pick = jax.random.fold_in(key, 8)
    light_most = max(3, NB // 3)
    counts = jax.random.randint(key_counts, (LEAVES,), 1, light_most + 1)
    chosen = jax.random.randint(key_pick, (), 0, LEAVES)
    counts = jnp.where(jnp.arange(LEAVES) == chosen, NB, counts)
    return counts.astype(jnp.int32)


def draw_near_count(key, part):
    return count_draw(key)


def draw_near_cols(key, part):
    counts = count_draw(key)
    key_scores = jax.random.fold_in(key, 13)
    positions = jnp.arange(GROUP, dtype=jnp.int32)
    leaf_ids = jnp.arange(LEAVES, dtype=jnp.int32)
    scores = jax.random.randint(key_scores, (LEAVES, GROUP), 0, 1 << 20) * GROUP + positions[None]
    own_offset = leaf_ids % GROUP
    scores = jnp.where(positions[None] == own_offset[:, None], -1, scores)
    order = jnp.argsort(scores, axis=1, stable=True)[:, :NB]
    columns = (leaf_ids // GROUP * GROUP)[:, None] + order
    slot_ids = jnp.arange(NB, dtype=jnp.int32)
    columns = jnp.where(slot_ids[None] < counts[:, None], columns, leaf_ids[:, None])
    return columns.astype(jnp.int32)


def draw_children(key, part):
    key_perm = jax.random.fold_in(key, 17)
    groups = LEAVES // GROUP
    half = GROUP // 2

    def one_perm(sub_key):
        return jax.random.permutation(sub_key, GROUP)
    perms = jax.vmap(one_perm)(jax.random.split(key_perm, groups))
    group_ids = jnp.arange(groups, dtype=jnp.int32)
    partner = group_ids + 1 - 2 * (group_ids % 2)
    first_kid = group_ids[:, None] * GROUP + perms[:, :half]
    second_kid = partner[:, None] * GROUP + perms[partner][:, half:]
    return jnp.stack([first_kid.reshape(-1), second_kid.reshape(-1)], axis=1).astype(jnp.int32)


def block_scale(own_key, dims, cuts, low, top_value):
    def one(position, shards_of):
        heights = jax.random.uniform(jax.random.fold_in(jax.random.fold_in(own_key, 6), position), (shards_of,), jnp.float32, low / len(cuts), top_value / len(cuts))
        return jnp.repeat(jnp.exp(heights), dims[position] // shards_of).reshape((-1,) + (1,) * (len(dims) - position - 1))

    factor_of = one(*cuts[0])
    for cut in cuts[1:]:
        factor_of = factor_of * one(*cut)
    return factor_of


def scatter_about(own_key, dims, scale, bound, pieces=(), kind=jnp.bfloat16):
    drawn = scale * jax.random.normal(own_key, dims, jnp.float32)
    if pieces:
        drawn = drawn * block_scale(own_key, dims, pieces, -0.22, 0.18)
    return jnp.clip(drawn, -bound, bound).astype(kind)


def setup_inputs(seed: int = 0) -> dict:
    streams_of = jax.random.split(jax.random.key(seed), 8)
    return {
        "near_blocks": draw_near_blocks(jax.random.fold_in(streams_of[7], 71), 0),
        "leaf_basis": draw_leaf_basis(jax.random.fold_in(streams_of[7], 71), 0),
        "near_cols": draw_near_cols(jax.random.fold_in(streams_of[7], 71), 0),
        "near_count": draw_near_count(jax.random.fold_in(streams_of[7], 71), 0),
        "children": draw_children(jax.random.fold_in(streams_of[7], 71), 0),
        "parent_basis": draw_parent_basis(jax.random.fold_in(streams_of[7], 71), 0),
        "far_coupling": scatter_about(streams_of[6], (PARENTS, RANK, RANK), (0.2 / RANK ** 0.5), 0.25, ((0, 32),), jnp.float32),
    }


HIGHEST = lax.Precision.HIGHEST

def rotate_pivot(near_block, basis):
    red_size = LEAF - RANK
    product = jnp.dot(near_block.astype(jnp.float32), basis.astype(jnp.float32), preferred_element_type=jnp.float32)
    rotated = jnp.dot(basis.astype(jnp.float32).T, product, precision=HIGHEST)
    factor = jnp.linalg.cholesky(rotated[:red_size, :red_size])
    pivot = jax.scipy.linalg.cho_solve((factor, True), rotated[:red_size, red_size:])
    self_schur = rotated[red_size:, red_size:] - jnp.dot(rotated[red_size:, :red_size], pivot, precision=HIGHEST)
    return (factor, pivot, self_schur)

def pair_schur(near_block, basis_own, pivot_own, basis_other, pivot_other):
    red_size = LEAF - RANK
    product = jnp.dot(near_block.astype(jnp.float32), basis_other.astype(jnp.float32), preferred_element_type=jnp.float32)
    own_float = basis_own.astype(jnp.float32)
    skel_rows = jnp.dot(own_float[:, red_size:].T, product, precision=HIGHEST)
    red_rows = jnp.dot(own_float[:, :red_size].T, product[:, red_size:], precision=HIGHEST)
    return skel_rows[:, red_size:] - jnp.dot(skel_rows[:, :red_size], pivot_other, precision=HIGHEST) - jnp.dot(pivot_own.T, red_rows, precision=HIGHEST)

def reference(near_blocks, leaf_basis, near_cols, near_count, children, parent_basis, far_coupling):

    def diag_part(pair_args):
        return rotate_pivot(pair_args[0], pair_args[1])
    factors, pivots, diag_schur = lax.map(diag_part, (near_blocks[:, 0], leaf_basis))
    slot_ids = jnp.arange(NB, dtype=jnp.int32)

    def leaf_row(row_args):
        blocks, leaf_id, columns, count = row_args

        def slot_term(slot_args):
            near_block, column = slot_args
            return pair_schur(near_block, leaf_basis[leaf_id], pivots[leaf_id], leaf_basis[column], pivots[column])
        terms = lax.map(slot_term, (blocks[1:], columns[1:]))
        schur_rows = jnp.concatenate([diag_schur[leaf_id][None], terms], axis=0)
        live = slot_ids < count
        return jnp.where(live[:, None, None], schur_rows, jnp.float32(0.0))
    near_schur = lax.map(leaf_row, (near_blocks, jnp.arange(LEAVES, dtype=jnp.int32), near_cols, near_count))

    def parent_part(parent_args):
        kids, basis, coupling = parent_args
        first_block = diag_schur[kids[0]]
        second_block = diag_schur[kids[1]]
        upper = jnp.concatenate([first_block, coupling], axis=1)
        lower = jnp.concatenate([coupling.T, second_block], axis=1)
        merged = jnp.concatenate([upper, lower], axis=0)
        basis_float = basis.astype(jnp.float32)
        rotated = jnp.dot(basis_float.T, jnp.dot(merged, basis_float, precision=HIGHEST), precision=HIGHEST)
        factor = jnp.linalg.cholesky(rotated[:RANK, :RANK])
        solved = jax.scipy.linalg.cho_solve((factor, True), rotated[:RANK, RANK:])
        top = rotated[RANK:, RANK:] - jnp.dot(rotated[RANK:, :RANK], solved, precision=HIGHEST)
        return (factor, top)
    top_factor, top_schur = lax.map(parent_part, (children, parent_basis, far_coupling))
    return (factors, near_schur, top_factor, top_schur)
```

```python
from functools import partial

import jax
import jax.numpy as jnp
from jax import lax
from jax.experimental import pallas as pl
from jax.experimental.pallas import tpu as pltpu
from jax.sharding import PartitionSpec as P

F32 = jnp.float32
BF16 = jnp.bfloat16
SUB = 8
NN = (((1,), (0,)), ((), ()))
NT = (((1,), (1,)), ((), ()))


def split(x):
    high = x.astype(BF16)
    return high, (x - high.astype(F32)).astype(BF16)


def mul(a, b, dims):
    return lax.dot_general(a, b, dims, preferred_element_type=F32)


def mul_three(a, b, dims):
    a_high, a_low = split(a)
    b_high, b_low = split(b)
    return mul(a_high, b_high, dims) + (mul(a_high, b_low, dims) + mul(a_low, b_high, dims))


def over_rows(x, k, width):
    return jnp.broadcast_to(x[k : k + 1, :], (SUB, width))


def factor_blocks(mats):
    order = mats[0].shape[0]
    count = order // SUB
    lane = lax.broadcasted_iota(jnp.int32, (SUB, order), 1)
    sub = lax.broadcasted_iota(jnp.int32, (SUB, order), 0)
    works = [[m[b * SUB : (b + 1) * SUB, :] for b in range(count)] for m in mats]
    uppers = [[] for _ in mats]
    inverses = [[] for _ in mats]
    for s in range(count):
        first = s * SUB
        inside = (lane >= first) & (lane < first + SUB)
        unit = jnp.where(lane == sub + first, F32(1.0), F32(0.0))
        columns = []
        pivots = []
        for work in works:
            columns.append(
                [
                    {
                        b: jnp.broadcast_to(work[b][:, first + n : first + n + 1], (SUB, order))
                        for b in range(s, count)
                    }
                    for n in range(SUB)
                ]
            )
            pivots.append(jnp.ones((SUB, order), F32))
            for b in range(s, count):
                work[b] = jnp.where(inside, unit if b == s else F32(0.0), work[b])
        for k in range(SUB):
            for which, work in enumerate(works):
                column = columns[which]
                pivot = over_rows(column[k][s], k, order)
                inverse = pl.reciprocal(pivot, approx=False)
                pivots[which] = jnp.where(sub == k, pivot, pivots[which])
                step = {b: column[k][b] * inverse for b in range(s, count)}
                step[s] = jnp.where(sub > k, step[s], F32(0.0))
                for n in range(k + 1, SUB):
                    value = over_rows(column[n][s], k, order)
                    for b in range(s, count):
                        column[n][b] = column[n][b] - step[b] * value
                row = over_rows(work[s], k, order)
                for b in range(s, count):
                    work[b] = work[b] - step[b] * row
        for which, work in enumerate(works):
            value = pivots[which]
            scale = lax.rsqrt(value)
            scale = scale * (F32(1.5) - F32(0.5) * value * scale * scale)
            upper = work[s]
            for n in range(SUB):
                upper = jnp.where(lane == first + n, columns[which][n][s], upper)
            upper = jnp.where(lane >= sub + first, upper, F32(0.0))
            uppers[which].append(upper * scale)
            inverses[which].append(
                jnp.where(lane <= sub + first, work[s], F32(0.0)) * scale
            )
    lowers = [jnp.concatenate(rows, axis=0).T for rows in uppers]
    inverse_lowers = [jnp.concatenate(rows, axis=0) for rows in inverses]
    return lowers, inverse_lowers


def leaf_kernel(near_ref, basis_ref, factor_ref, schur_ref, rows_ref, work, inv, turned):
    leaves = basis_ref.shape[0]
    block = schur_ref.shape[1]
    parts = basis_ref.shape[1] // block
    red = parts - 1
    for leaf in range(leaves):
        basis = basis_ref[leaf]
        turned[leaf] = basis.T
        high, low = split(mul(near_ref[leaf, 0], basis, NN))
        for i in range(parts):
            left = turned[leaf, i * block : (i + 1) * block, :]
            for j in range(i + 1):
                cut = slice(j * block, (j + 1) * block)
                work[leaf, i, j] = mul(left, high[:, cut], NN) + mul(left, low[:, cut], NN)
        for i in range(red):
            for j in range(i + 1, red):
                factor_ref[
                    leaf, i * block : (i + 1) * block, j * block : (j + 1) * block
                ] = jnp.zeros((block, block), F32)

    def eliminate(k, _):
        lowers, inverses = factor_blocks([work[leaf, k, k] for leaf in range(leaves)])
        for leaf in range(leaves):
            work[leaf, k, k] = lowers[leaf]
            inv[leaf, k] = inverses[leaf]
        for i in range(1, parts):

            @pl.when(i > k)
            def _(i=i):
                for leaf in range(leaves):
                    work[leaf, i, k] = mul_three(work[leaf, i, k], inv[leaf, k], NT)

        for i in range(1, parts):
            for j in range(1, i + 1):

                @pl.when(j > k)
                def _(i=i, j=j):
                    for leaf in range(leaves):
                        work[leaf, i, j] = work[leaf, i, j] - mul_three(
                            work[leaf, i, k], work[leaf, j, k], NT
                        )

        return 0

    lax.fori_loop(0, red, eliminate, 0)
    for leaf in range(leaves):
        for i in range(red):
            for j in range(i + 1):
                factor_ref[
                    leaf, i * block : (i + 1) * block, j * block : (j + 1) * block
                ] = work[leaf, i, j]
        schur_ref[leaf] = work[leaf, red, red]
        solved = {}
        total = jnp.zeros((block, basis_ref.shape[1]), F32)
        for k in reversed(range(red)):
            value = work[leaf, red, k]
            for m in range(k + 1, red):
                value = value - mul_three(solved[m], work[leaf, m, k], NN)
            solved[k] = mul_three(value, inv[leaf, k], NN)
            high, low = split(solved[k])
            right = turned[leaf, k * block : (k + 1) * block, :]
            total = total + (mul(high, right, NN) + mul(low, right, NN))
        rows_ref[leaf, :block, :] = turned[leaf, red * block :, :]
        rows_ref[leaf, block:, :] = total.astype(BF16)


def leaf_stage(near_blocks, leaf_basis, block):
    leaves, size = leaf_basis.shape[:2]
    red_size = size - block
    parts = size // block
    return pl.pallas_call(
        leaf_kernel,
        grid=(1,),
        in_specs=[
            pl.BlockSpec((leaves, 1, size, size), lambda g: (0, 0, 0, 0)),
            pl.BlockSpec((leaves, size, size), lambda g: (0, 0, 0)),
        ],
        out_specs=[
            pl.BlockSpec((leaves, red_size, red_size), lambda g: (0, 0, 0)),
            pl.BlockSpec((leaves, block, block), lambda g: (0, 0, 0)),
            pl.BlockSpec((leaves, 2 * block, size), lambda g: (0, 0, 0)),
        ],
        out_shape=[
            jax.ShapeDtypeStruct((leaves, red_size, red_size), F32),
            jax.ShapeDtypeStruct((leaves, block, block), F32),
            jax.ShapeDtypeStruct((leaves, 2 * block, size), BF16),
        ],
        scratch_shapes=[
            pltpu.VMEM((leaves, parts, parts, block, block), F32),
            pltpu.VMEM((leaves, parts - 1, block, block), F32),
            pltpu.VMEM((leaves, size, size), BF16),
        ],
        compiler_params=pltpu.CompilerParams(vmem_limit_bytes=40 << 20),
        cost_estimate=pl.CostEstimate(
            flops=40_000_000_000, bytes_accessed=6_000_000, transcendentals=0
        ),
        name="leaf_stage",
    )(near_blocks, leaf_basis)


DEPTH = 4


def near_kernel(
    cols_ref, count_ref, base_ref, near_ref, own_ref, skel_ref, turned_ref, diag_ref, out_ref, buf, sems
):
    leaves = own_ref.shape[0]
    block = diag_ref.shape[1]
    first = count_ref[0] - 1
    total = first
    for leaf in range(1, leaves):
        total = total + count_ref[leaf] - 1

    def place(w):
        leaf = jnp.int32(0)
        slot = w
        for other in range(leaves - 1):
            span = count_ref[other] - 1
            past = (leaf == other) & (slot >= span)
            slot = jnp.where(past, slot - span, slot)
            leaf = jnp.where(past, leaf + 1, leaf)
        return leaf, slot + 1

    def copy_of(w):
        leaf, slot = place(w)
        at = lax.rem(w, DEPTH)
        return pltpu.make_async_copy(near_ref.at[leaf, slot], buf.at[at], sems.at[at])

    for w in range(DEPTH - 1):

        @pl.when(w < total)
        def _(w=w):
            copy_of(jnp.int32(w)).start()

    out_ref[...] = jnp.zeros_like(out_ref)
    for leaf in range(leaves):
        out_ref[leaf, 0] = diag_ref[leaf]

    def body(w, _):
        @pl.when(w + DEPTH - 1 < total)
        def _():
            copy_of(w + DEPTH - 1).start()

        copy_of(w).wait()
        leaf, slot = place(w)
        other = cols_ref[leaf, slot] - base_ref[0]
        left = mul(own_ref[leaf], buf[lax.rem(w, DEPTH)], NN)
        skel_rows = left[:block]
        mixed = (skel_rows - left[block:]).astype(BF16)
        out_ref[leaf, slot] = mul(mixed, skel_ref[other], NN) - mul(
            skel_rows.astype(BF16), turned_ref[other], NT
        )
        return 0

    lax.fori_loop(0, total, body, 0)


def near_stage(near_blocks, near_cols, near_count, base, own_rows, skel, turned, diag):
    leaves, slots = near_cols.shape
    size = near_blocks.shape[2]
    block = diag.shape[1]
    whole = pl.BlockSpec(memory_space=pltpu.VMEM)
    scalar = pl.BlockSpec(memory_space=pltpu.SMEM)
    return pl.pallas_call(
        near_kernel,
        in_specs=[scalar, scalar, scalar, pl.BlockSpec(memory_space=pl.ANY), whole, whole, whole, whole],
        out_specs=whole,
        out_shape=jax.ShapeDtypeStruct((leaves, slots, block, block), F32),
        scratch_shapes=[
            pltpu.VMEM((DEPTH, size, size), BF16),
            pltpu.SemaphoreType.DMA((DEPTH,)),
        ],
        compiler_params=pltpu.CompilerParams(vmem_limit_bytes=40 << 20),
        name="near_stage",
    )(near_cols, near_count, base, near_blocks, own_rows, skel, turned, diag)


def top_kernel(first_ref, second_ref, coupling_ref, basis_ref, factor_ref, schur_ref, merged, rotated):
    block = first_ref.shape[0]
    merged[:block, :block] = first_ref[...]
    merged[:block, block:] = coupling_ref[...]
    merged[block:, :block] = coupling_ref[...].T
    merged[block:, block:] = second_ref[...]
    basis = basis_ref[...]
    high, low = split(merged[...])
    high, low = split(mul(high, basis, NN) + mul(low, basis, NN))
    left = basis.T
    rotated[...] = mul(left, high, NN) + mul(left, low, NN)
    lowers, inverses = factor_blocks([rotated[:block, :block]])
    factor_ref[...] = lowers[0]
    tail = mul_three(rotated[block:, :block], inverses[0], NT)
    schur_ref[...] = rotated[block:, block:] - mul_three(tail, tail, NT)


def top_stage(first_block, second_block, coupling, basis):
    block = coupling.shape[0]
    whole = pl.BlockSpec(memory_space=pltpu.VMEM)
    return pl.pallas_call(
        top_kernel,
        in_specs=[whole] * 4,
        out_specs=[whole] * 2,
        out_shape=[jax.ShapeDtypeStruct((block, block), F32)] * 2,
        scratch_shapes=[
            pltpu.VMEM((2 * block, 2 * block), F32),
            pltpu.VMEM((2 * block, 2 * block), F32),
        ],
        cost_estimate=pl.CostEstimate(
            flops=10_000_000_000, bytes_accessed=600_000, transcendentals=0
        ),
        name="top_stage",
    )(first_block, second_block, coupling, basis)


def local(near_blocks, leaf_basis, near_cols, near_count, children, parent_basis, far_coupling):
    local_leaves = near_cols.shape[0]
    block = far_coupling.shape[1]
    red_size = leaf_basis.shape[1] - block
    row_index = lax.axis_index("row")
    col_index = lax.axis_index("col")
    col_count = lax.axis_size("col")
    row_count = lax.axis_size("row")
    group_size = local_leaves * col_count
    group_base = row_index * group_size
    skel = lax.all_gather(leaf_basis[:, :, red_size:], "col", axis=0, tiled=True)
    factors, diag_schur, rows = leaf_stage(near_blocks, leaf_basis, block)
    child_all = lax.all_gather(diag_schur, "col", axis=0, tiled=True)
    turned = lax.all_gather(rows[:, block:, :], "col", axis=0, tiled=True)
    partner_row = row_index + 1 - 2 * (row_index % 2)
    parent_id = row_index * col_count + col_index
    first_block = child_all[children[parent_id, 0] - group_base]
    partner_parent = partner_row * col_count + col_index
    outgoing = child_all[children[partner_parent, 1] - group_base]
    route = [(r, r ^ 1) for r in range(row_count)]
    second_block = lax.ppermute(outgoing, "row", route)
    top_factor, top_schur = top_stage(first_block, second_block, far_coupling[0], parent_basis[0])
    base = jnp.reshape(group_base, (1,)).astype(jnp.int32)
    near_schur = near_stage(
        near_blocks, near_cols, near_count, base, rows, skel, turned, diag_schur
    )
    return (factors, near_schur, top_factor[None], top_schur[None])


def solution(mesh):
    placed = (
        P(("row", "col"), None, None, None),
        P(("row", "col"), None, None),
        P(("row", "col"), None),
        P(("row", "col")),
        P(),
        P(("row", "col"), None, None),
        P(("row", "col"), None, None),
    )
    return jax.shard_map(
        local,
        mesh=mesh,
        in_specs=placed,
        out_specs=(
            P(("row", "col"), None, None),
            P(("row", "col"), None, None, None),
            P(("row", "col"), None, None),
            P(("row", "col"), None, None),
        ),
        check_vma=False,
    )
```

```python
from functools import partial

import jax
import jax.numpy as jnp
from jax import lax
from jax.experimental import pallas as pl
from jax.experimental.pallas import tpu as pltpu
from jax.sharding import PartitionSpec as P

F32 = jnp.float32
BF16 = jnp.bfloat16
SUB = 8
NN = (((1,), (0,)), ((), ()))
NT = (((1,), (1,)), ((), ()))


def split(x):
    high = x.astype(BF16)
    return high, (x - high.astype(F32)).astype(BF16)


def mul(a, b, dims):
    return lax.dot_general(a, b, dims, preferred_element_type=F32)


def mul_three(a, b, dims):
    a_high, a_low = split(a)
    b_high, b_low = split(b)
    return mul(a_high, b_high, dims) + (mul(a_high, b_low, dims) + mul(a_low, b_high, dims))


def over_rows(x, k, width):
    return jnp.broadcast_to(x[k : k + 1, :], (SUB, width))


def factor_blocks(mats):
    order = mats[0].shape[0]
    count = order // SUB
    lane = lax.broadcasted_iota(jnp.int32, (SUB, order), 1)
    sub = lax.broadcasted_iota(jnp.int32, (SUB, order), 0)
    works = [[m[b * SUB : (b + 1) * SUB, :] for b in range(count)] for m in mats]
    uppers = [[] for _ in mats]
    inverses = [[] for _ in mats]
    for s in range(count):
        first = s * SUB
        inside = (lane >= first) & (lane < first + SUB)
        unit = jnp.where(lane == sub + first, F32(1.0), F32(0.0))
        columns = []
        pivots = []
        for work in works:
            columns.append(
                [
                    {
                        b: jnp.broadcast_to(work[b][:, first + n : first + n + 1], (SUB, order))
                        for b in range(s, count)
                    }
                    for n in range(SUB)
                ]
            )
            pivots.append(jnp.ones((SUB, order), F32))
            for b in range(s, count):
                work[b] = jnp.where(inside, unit if b == s else F32(0.0), work[b])
        for k in range(SUB):
            for which, work in enumerate(works):
                column = columns[which]
                pivot = over_rows(column[k][s], k, order)
                inverse = pl.reciprocal(pivot, approx=False)
                pivots[which] = jnp.where(sub == k, pivot, pivots[which])
                step = {b: column[k][b] * inverse for b in range(s, count)}
                step[s] = jnp.where(sub > k, step[s], F32(0.0))
                for n in range(k + 1, SUB):
                    value = over_rows(column[n][s], k, order)
                    for b in range(s, count):
                        column[n][b] = column[n][b] - step[b] * value
                row = over_rows(work[s], k, order)
                for b in range(s, count):
                    work[b] = work[b] - step[b] * row
        for which, work in enumerate(works):
            value = pivots[which]
            scale = lax.rsqrt(value)
            scale = scale * (F32(1.5) - F32(0.5) * value * scale * scale)
            upper = work[s]
            for n in range(SUB):
                upper = jnp.where(lane == first + n, columns[which][n][s], upper)
            upper = jnp.where(lane >= sub + first, upper, F32(0.0))
            uppers[which].append(upper * scale)
            inverses[which].append(
                jnp.where(lane <= sub + first, work[s], F32(0.0)) * scale
            )
    lowers = [jnp.concatenate(rows, axis=0).T for rows in uppers]
    inverse_lowers = [jnp.concatenate(rows, axis=0) for rows in inverses]
    return lowers, inverse_lowers


def leaf_kernel(near_ref, basis_ref, factor_ref, schur_ref, skel_ref, rows_ref, work, inv, turned):
    leaves = basis_ref.shape[0]
    block = schur_ref.shape[1]
    parts = basis_ref.shape[1] // block
    red = parts - 1
    for leaf in range(leaves):
        basis = basis_ref[leaf]
        turned[leaf] = basis.T
        high, low = split(mul(near_ref[leaf, 0], basis, NN))
        for i in range(parts):
            left = turned[leaf, i * block : (i + 1) * block, :]
            for j in range(i + 1):
                cut = slice(j * block, (j + 1) * block)
                work[leaf, i, j] = mul(left, high[:, cut], NN) + mul(left, low[:, cut], NN)
        for i in range(red):
            for j in range(i + 1, red):
                factor_ref[
                    leaf, i * block : (i + 1) * block, j * block : (j + 1) * block
                ] = jnp.zeros((block, block), F32)

    def eliminate(k, _):
        lowers, inverses = factor_blocks([work[leaf, k, k] for leaf in range(leaves)])
        for leaf in range(leaves):
            work[leaf, k, k] = lowers[leaf]
            inv[leaf, k] = inverses[leaf]
        for i in range(1, parts):

            @pl.when(i > k)
            def _(i=i):
                for leaf in range(leaves):
                    work[leaf, i, k] = mul_three(work[leaf, i, k], inv[leaf, k], NT)

        for i in range(1, parts):
            for j in range(1, i + 1):

                @pl.when(j > k)
                def _(i=i, j=j):
                    for leaf in range(leaves):
                        work[leaf, i, j] = work[leaf, i, j] - mul_three(
                            work[leaf, i, k], work[leaf, j, k], NT
                        )

        return 0

    lax.fori_loop(0, red, eliminate, 0)
    for leaf in range(leaves):
        for i in range(red):
            for j in range(i + 1):
                factor_ref[
                    leaf, i * block : (i + 1) * block, j * block : (j + 1) * block
                ] = work[leaf, i, j]
        schur_ref[leaf] = work[leaf, red, red]
        solved = {}
        total = jnp.zeros((block, basis_ref.shape[1]), F32)
        for k in reversed(range(red)):
            value = work[leaf, red, k]
            for m in range(k + 1, red):
                value = value - mul_three(solved[m], work[leaf, m, k], NN)
            solved[k] = mul_three(value, inv[leaf, k], NN)
            high, low = split(solved[k])
            right = turned[leaf, k * block : (k + 1) * block, :]
            total = total + (mul(high, right, NN) + mul(low, right, NN))
        skel_ref[leaf] = turned[leaf, red * block :, :]
        rows_ref[leaf] = total.astype(BF16)


def leaf_stage(near_blocks, leaf_basis, block):
    leaves, size = leaf_basis.shape[:2]
    red_size = size - block
    parts = size // block
    return pl.pallas_call(
        leaf_kernel,
        grid=(1,),
        in_specs=[
            pl.BlockSpec((leaves, 1, size, size), lambda g: (0, 0, 0, 0)),
            pl.BlockSpec((leaves, size, size), lambda g: (0, 0, 0)),
        ],
        out_specs=[
            pl.BlockSpec((leaves, red_size, red_size), lambda g: (0, 0, 0)),
            pl.BlockSpec((leaves, block, block), lambda g: (0, 0, 0)),
            pl.BlockSpec((leaves, block, size), lambda g: (0, 0, 0)),
            pl.BlockSpec((leaves, block, size), lambda g: (0, 0, 0)),
        ],
        out_shape=[
            jax.ShapeDtypeStruct((leaves, red_size, red_size), F32),
            jax.ShapeDtypeStruct((leaves, block, block), F32),
            jax.ShapeDtypeStruct((leaves, block, size), BF16),
            jax.ShapeDtypeStruct((leaves, block, size), BF16),
        ],
        scratch_shapes=[
            pltpu.VMEM((leaves, parts, parts, block, block), F32),
            pltpu.VMEM((leaves, parts - 1, block, block), F32),
            pltpu.VMEM((leaves, size, size), BF16),
        ],
        compiler_params=pltpu.CompilerParams(vmem_limit_bytes=40 << 20),
        cost_estimate=pl.CostEstimate(
            flops=40_000_000_000, bytes_accessed=6_000_000, transcendentals=0
        ),
        name="leaf_stage",
    )(near_blocks, leaf_basis)


DEPTH = 4


def near_kernel(
    cols_ref, count_ref, place_ref, near_ref, own_ref, own_turned_ref, turned_ref, diag_ref, *rest
):
    devices = turned_ref.shape[0]
    skel_refs = rest[:devices]
    out_ref, skel, left_rows, buf, sems, skel_sems = rest[devices:]
    skel_copies = [
        pltpu.make_async_copy(skel_refs[d], skel.at[d], skel_sems.at[d]) for d in range(devices)
    ]
    leaves = own_ref.shape[0]
    block = diag_ref.shape[1]
    first = count_ref[0] - 1
    total = first
    for leaf in range(1, leaves):
        total = total + count_ref[leaf] - 1

    def place(w):
        leaf = jnp.int32(0)
        slot = w
        for other in range(leaves - 1):
            span = count_ref[other] - 1
            past = (leaf == other) & (slot >= span)
            slot = jnp.where(past, slot - span, slot)
            leaf = jnp.where(past, leaf + 1, leaf)
        return leaf, slot + 1

    def copy_of(w):
        leaf, slot = place(w)
        at = lax.rem(w, DEPTH)
        return pltpu.make_async_copy(near_ref.at[leaf, slot], buf.at[at], sems.at[at])

    for w in range(DEPTH - 1):

        @pl.when(w < total)
        def _(w=w):
            copy_of(jnp.int32(w)).start()

    for copy in skel_copies:
        copy.start()
    out_ref[...] = jnp.zeros_like(out_ref)
    for leaf in range(leaves):
        out_ref[leaf, 0] = diag_ref[leaf]
        left_rows[leaf, :block, :] = own_ref[leaf]
        left_rows[leaf, block:, :] = own_turned_ref[leaf]
    for copy in skel_copies:
        copy.wait()

    def body(w, _):
        @pl.when(w + DEPTH - 1 < total)
        def _():
            copy_of(w + DEPTH - 1).start()

        copy_of(w).wait()
        leaf, slot = place(w)
        other = cols_ref[leaf, slot] - place_ref[0]
        device = other // leaves
        inner = other - device * leaves
        distance = lax.rem(place_ref[1] - device + devices, devices)
        left = mul(left_rows[leaf], buf[lax.rem(w, DEPTH)], NN)
        skel_rows = left[:block]
        mixed = (skel_rows - left[block:]).astype(BF16)
        out_ref[leaf, slot] = mul(mixed, skel[distance, inner], NN) - mul(
            skel_rows.astype(BF16), turned_ref[device, inner], NT
        )
        return 0

    lax.fori_loop(0, total, body, 0)


def near_stage(near_blocks, near_cols, near_count, place, own_skel, own_turned, turned, diag, skels):
    leaves, slots = near_cols.shape
    size = near_blocks.shape[2]
    block = diag.shape[1]
    devices = len(skels)
    whole = pl.BlockSpec(memory_space=pltpu.VMEM)
    scalar = pl.BlockSpec(memory_space=pltpu.SMEM)
    left = pl.BlockSpec(memory_space=pl.ANY)
    return pl.pallas_call(
        near_kernel,
        in_specs=[scalar] * 3 + [left] + [whole] * 4 + [left] * devices,
        out_specs=whole,
        out_shape=jax.ShapeDtypeStruct((leaves, slots, block, block), F32),
        scratch_shapes=[
            pltpu.VMEM((devices, leaves, size, block), BF16),
            pltpu.VMEM((leaves, 2 * block, size), BF16),
            pltpu.VMEM((DEPTH, size, size), BF16),
            pltpu.SemaphoreType.DMA((DEPTH,)),
            pltpu.SemaphoreType.DMA((devices,)),
        ],
        compiler_params=pltpu.CompilerParams(vmem_limit_bytes=40 << 20),
        name="near_stage",
    )(near_cols, near_count, place, near_blocks, own_skel, own_turned, turned, diag, *skels)


def exchange_kernel(
    count, depth, schur_ref, turned_ref, schur_all, turned_all, own_sem, send_z, recv_z, send_x, recv_x
):
    width = count // depth
    me = lax.axis_index("col")
    z = me // width
    x = me % width
    away = sorted(range(1, depth), key=lambda d: min(d, depth - d))
    across = range(1, width)

    def along_z(d):
        return ((z + d) % depth) * width + x

    def along_x(e):
        return z * width + (x + e) % width

    barrier = pltpu.get_barrier_semaphore()
    for d in away:
        pl.semaphore_signal(barrier, inc=1, device_id={"col": along_z(d)})
    for e in across:
        pl.semaphore_signal(barrier, inc=1, device_id={"col": along_x(e)})
    pl.semaphore_wait(barrier, depth - 1 + width - 1)
    pairs = ((schur_ref, schur_all), (turned_ref, turned_all))
    started = []
    own = []
    for q, (source, target) in enumerate(pairs):
        for d in away:
            started.append(
                pltpu.make_async_remote_copy(
                    src_ref=source,
                    dst_ref=target.at[me],
                    send_sem=send_z.at[q, d],
                    recv_sem=recv_z.at[q, d],
                    device_id={"col": along_z(d)},
                )
            )
            started[-1].start()
        for e in across:
            started.append(
                pltpu.make_async_remote_copy(
                    src_ref=source,
                    dst_ref=target.at[me],
                    send_sem=send_x.at[q, 0, e],
                    recv_sem=recv_x.at[q, 0, e],
                    device_id={"col": along_x(e)},
                )
            )
            started[-1].start()
        own.append(pltpu.make_async_copy(source, target.at[me], own_sem.at[q]))
        own[-1].start()
    for q, (source, target) in enumerate(pairs):
        for d in away:
            block = along_z(depth - d)
            pltpu.make_async_remote_copy(
                src_ref=target.at[block],
                dst_ref=target.at[block],
                send_sem=send_z.at[q, d],
                recv_sem=recv_z.at[q, d],
                device_id={"col": block},
            ).wait_recv()
            for e in across:
                started.append(
                    pltpu.make_async_remote_copy(
                        src_ref=target.at[block],
                        dst_ref=target.at[block],
                        send_sem=send_x.at[q, d, e],
                        recv_sem=recv_x.at[q, d, e],
                        device_id={"col": along_x(e)},
                    )
                )
                started[-1].start()
    for q, (source, target) in enumerate(pairs):
        for d in [0] + away:
            for e in across:
                block = ((z + depth - d) % depth) * width + (x + width - e) % width
                pltpu.make_async_remote_copy(
                    src_ref=target.at[block],
                    dst_ref=target.at[block],
                    send_sem=send_x.at[q, d, e],
                    recv_sem=recv_x.at[q, d, e],
                    device_id={"col": along_x(width - e)},
                ).wait_recv()
    for copy in started:
        copy.wait_send()
    for copy in own:
        copy.wait()


def exchange(schur, turned, count):
    depth = 4 if count % 4 == 0 else count
    width = count // depth
    left = pl.BlockSpec(memory_space=pl.ANY)
    return pl.pallas_call(
        partial(exchange_kernel, count, depth),
        in_specs=[left] * 2,
        out_specs=[left] * 2,
        out_shape=[
            jax.ShapeDtypeStruct((count,) + schur.shape, schur.dtype),
            jax.ShapeDtypeStruct((count,) + turned.shape, turned.dtype),
        ],
        scratch_shapes=[
            pltpu.SemaphoreType.DMA((2,)),
            pltpu.SemaphoreType.DMA((2, depth)),
            pltpu.SemaphoreType.DMA((2, depth)),
            pltpu.SemaphoreType.DMA((2, depth, width)),
            pltpu.SemaphoreType.DMA((2, depth, width)),
        ],
        compiler_params=pltpu.CompilerParams(collective_id=0, has_side_effects=True),
        cost_estimate=pl.CostEstimate(flops=0, bytes_accessed=60_000_000, transcendentals=0),
        name="exchange",
    )(schur, turned)


def top_kernel(first_ref, second_ref, coupling_ref, basis_ref, factor_ref, schur_ref, merged, rotated):
    block = first_ref.shape[0]
    merged[:block, :block] = first_ref[...]
    merged[:block, block:] = coupling_ref[...]
    merged[block:, :block] = coupling_ref[...].T
    merged[block:, block:] = second_ref[...]
    basis = basis_ref[...]
    high, low = split(merged[...])
    high, low = split(mul(high, basis, NN) + mul(low, basis, NN))
    left = basis.T
    rotated[...] = mul(left, high, NN) + mul(left, low, NN)
    lowers, inverses = factor_blocks([rotated[:block, :block]])
    factor_ref[...] = lowers[0]
    tail = mul_three(rotated[block:, :block], inverses[0], NT)
    schur_ref[...] = rotated[block:, block:] - mul_three(tail, tail, NT)


def top_stage(first_block, second_block, coupling, basis):
    block = coupling.shape[0]
    whole = pl.BlockSpec(memory_space=pltpu.VMEM)
    return pl.pallas_call(
        top_kernel,
        in_specs=[whole] * 4,
        out_specs=[whole] * 2,
        out_shape=[jax.ShapeDtypeStruct((block, block), F32)] * 2,
        scratch_shapes=[
            pltpu.VMEM((2 * block, 2 * block), F32),
            pltpu.VMEM((2 * block, 2 * block), F32),
        ],
        cost_estimate=pl.CostEstimate(
            flops=10_000_000_000, bytes_accessed=600_000, transcendentals=0
        ),
        name="top_stage",
    )(first_block, second_block, coupling, basis)


def local(near_blocks, leaf_basis, near_cols, near_count, children, parent_basis, far_coupling):
    local_leaves = near_cols.shape[0]
    block = far_coupling.shape[1]
    red_size = leaf_basis.shape[1] - block
    row_index = lax.axis_index("row")
    col_index = lax.axis_index("col")
    col_count = lax.axis_size("col")
    row_count = lax.axis_size("row")
    group_size = local_leaves * col_count
    group_base = row_index * group_size
    skel = leaf_basis[:, :, red_size:]
    skels = [skel] + [
        lax.ppermute(skel, "col", [(c, (c + s) % col_count) for c in range(col_count)])
        for s in range(1, col_count)
    ]
    factors, diag_schur, own_skel, own_turned = leaf_stage(near_blocks, leaf_basis, block)
    child_all, turned = exchange(diag_schur, own_turned, col_count)
    child_all = child_all.reshape(group_size, block, block)
    partner_row = row_index + 1 - 2 * (row_index % 2)
    parent_id = row_index * col_count + col_index
    first_block = child_all[children[parent_id, 0] - group_base]
    partner_parent = partner_row * col_count + col_index
    outgoing = child_all[children[partner_parent, 1] - group_base]
    route = [(r, r ^ 1) for r in range(row_count)]
    second_block = lax.ppermute(outgoing, "row", route)
    top_factor, top_schur = top_stage(first_block, second_block, far_coupling[0], parent_basis[0])
    place = jnp.stack([group_base, col_index]).astype(jnp.int32)
    near_schur = near_stage(
        near_blocks, near_cols, near_count, place, own_skel, own_turned, turned, diag_schur, skels
    )
    return (factors, near_schur, top_factor[None], top_schur[None])


def solution(mesh):
    placed = (
        P(("row", "col"), None, None, None),
        P(("row", "col"), None, None),
        P(("row", "col"), None),
        P(("row", "col")),
        P(),
        P(("row", "col"), None, None),
        P(("row", "col"), None, None),
    )
    return jax.shard_map(
        local,
        mesh=mesh,
        in_specs=placed,
        out_specs=(
            P(("row", "col"), None, None),
            P(("row", "col"), None, None, None),
            P(("row", "col"), None, None),
            P(("row", "col"), None, None),
        ),
        check_vma=False,
    )
```

```python
from functools import partial

import jax
import jax.numpy as jnp
from jax import lax
from jax.experimental import pallas as pl
from jax.experimental.pallas import tpu as pltpu
from jax.sharding import PartitionSpec as P

F32 = jnp.float32
BF16 = jnp.bfloat16
SUB = 8
WIDE = 4
NN = (((1,), (0,)), ((), ()))
NT = (((1,), (1,)), ((), ()))


def split(x):
    high = x.astype(BF16)
    return high, (x - high.astype(F32)).astype(BF16)


def mul(a, b, dims):
    return lax.dot_general(a, b, dims, preferred_element_type=F32)


def mul_three(a, b, dims):
    a_high, a_low = split(a)
    b_high, b_low = split(b)
    return mul(a_high, b_high, dims) + (mul(a_high, b_low, dims) + mul(a_low, b_high, dims))


def over_rows(x, k, width):
    return jnp.broadcast_to(x[k : k + 1, :], (SUB, width))


def pack(x):
    half = x.shape[0] // 2
    down = lax.broadcasted_iota(jnp.int32, (half, half), 0)
    right = lax.broadcasted_iota(jnp.int32, (half, half), 1)
    last = x[half:, half:]
    both = jnp.where(down >= right, x[:half, :half], last)
    main = jnp.sum(jnp.where(down == right, last, F32(0.0)), axis=0, keepdims=True)
    main = jnp.broadcast_to(main, (SUB, half))
    return jnp.concatenate(
        [
            jnp.concatenate([x[half:, :half], both], axis=1),
            jnp.concatenate([main, main], axis=1),
        ],
        axis=0,
    )


def unpack(packed):
    half = packed.shape[0] - SUB
    down = lax.broadcasted_iota(jnp.int32, (half, half), 0)
    right = lax.broadcasted_iota(jnp.int32, (half, half), 1)
    corner = packed[:half, :half]
    both = packed[:half, half:]
    turned = both.T
    main = jnp.broadcast_to(packed[half : half + 1, :half], (half, half))
    begin = jnp.where(down >= right, both, turned)
    end = jnp.where(down < right, both, turned)
    end = jnp.where(down == right, main, end)
    return begin, corner, end


def factor_blocks(mats):
    order = mats[0].shape[0]
    count = order // SUB
    lane = lax.broadcasted_iota(jnp.int32, (SUB, order), 1)
    sub = lax.broadcasted_iota(jnp.int32, (SUB, order), 0)
    works = [[m[b * SUB : (b + 1) * SUB, :] for b in range(count)] for m in mats]
    uppers = [[] for _ in mats]
    inverses = [[] for _ in mats]
    for s in range(count):
        start = s * SUB
        pivots = [jnp.ones((SUB, order), F32) for _ in mats]
        seen = [[] for _ in mats]
        for first in range(start, start + SUB, WIDE):
            inside = (lane >= first) & (lane < first + WIDE)
            unit = jnp.where(lane == sub + start, F32(1.0), F32(0.0))
            columns = []
            for work in works:
                columns.append(
                    [
                        {
                            b: jnp.broadcast_to(work[b][:, first + n : first + n + 1], (SUB, order))
                            for b in range(s, count)
                        }
                        for n in range(WIDE)
                    ]
                )
                for b in range(s, count):
                    work[b] = jnp.where(inside, unit if b == s else F32(0.0), work[b])
            for m in range(WIDE):
                k = first - start + m
                for which, work in enumerate(works):
                    column = columns[which]
                    pivot = over_rows(column[m][s], k, order)
                    inverse = pl.reciprocal(pivot, approx=False)
                    pivots[which] = jnp.where(sub == k, pivot, pivots[which])
                    step = {b: column[m][b] * inverse for b in range(s, count)}
                    step[s] = jnp.where(sub > k, step[s], F32(0.0))
                    for n in range(m + 1, WIDE):
                        value = over_rows(column[n][s], k, order)
                        for b in range(s, count):
                            column[n][b] = column[n][b] - step[b] * value
                    row = over_rows(work[s], k, order)
                    for b in range(s, count):
                        work[b] = work[b] - step[b] * row
            for which in range(len(mats)):
                seen[which] += [column[s] for column in columns[which]]
        for which, work in enumerate(works):
            value = pivots[which]
            scale = lax.rsqrt(value)
            scale = scale * (F32(1.5) - F32(0.5) * value * scale * scale)
            upper = work[s]
            for n in range(SUB):
                upper = jnp.where(lane == start + n, seen[which][n], upper)
            upper = jnp.where(lane >= sub + start, upper, F32(0.0))
            uppers[which].append(upper * scale)
            inverses[which].append(
                jnp.where(lane <= sub + start, work[s], F32(0.0)) * scale
            )
    lowers = [jnp.concatenate(rows, axis=0).T for rows in uppers]
    inverse_lowers = [jnp.concatenate(rows, axis=0) for rows in inverses]
    return lowers, inverse_lowers


def leaf_kernel(near_ref, basis_ref, factor_ref, schur_ref, packed_ref, skel_ref, rows_ref, work, inv, turned):
    leaves = basis_ref.shape[0]
    block = schur_ref.shape[1]
    parts = basis_ref.shape[1] // block
    red = parts - 1
    for leaf in range(leaves):
        basis = basis_ref[leaf]
        turned[leaf] = basis.T
        high, low = split(mul(near_ref[leaf, 0], basis, NN))
        for i in range(parts):
            left = turned[leaf, i * block : (i + 1) * block, :]
            for j in range(i + 1):
                cut = slice(j * block, (j + 1) * block)
                work[leaf, i, j] = mul(left, high[:, cut], NN) + mul(left, low[:, cut], NN)
        for i in range(red):
            for j in range(i + 1, red):
                factor_ref[
                    leaf, i * block : (i + 1) * block, j * block : (j + 1) * block
                ] = jnp.zeros((block, block), F32)

    def eliminate(k, _):
        lowers, inverses = factor_blocks([work[leaf, k, k] for leaf in range(leaves)])
        for leaf in range(leaves):
            work[leaf, k, k] = lowers[leaf]
            inv[leaf, k] = inverses[leaf]
        for i in range(1, parts):

            @pl.when(i > k)
            def _(i=i):
                for leaf in range(leaves):
                    work[leaf, i, k] = mul_three(work[leaf, i, k], inv[leaf, k], NT)

        for i in range(1, parts):
            for j in range(1, i + 1):

                @pl.when(j > k)
                def _(i=i, j=j):
                    for leaf in range(leaves):
                        work[leaf, i, j] = work[leaf, i, j] - mul_three(
                            work[leaf, i, k], work[leaf, j, k], NT
                        )

        return 0

    lax.fori_loop(0, red, eliminate, 0)
    for leaf in range(leaves):
        for i in range(red):
            for j in range(i + 1):
                factor_ref[
                    leaf, i * block : (i + 1) * block, j * block : (j + 1) * block
                ] = work[leaf, i, j]
        schur_ref[leaf] = work[leaf, red, red]
        packed_ref[leaf] = pack(work[leaf, red, red])
        solved = {}
        total = jnp.zeros((block, basis_ref.shape[1]), F32)
        for k in reversed(range(red)):
            value = work[leaf, red, k]
            for m in range(k + 1, red):
                value = value - mul_three(solved[m], work[leaf, m, k], NN)
            solved[k] = mul_three(value, inv[leaf, k], NN)
            high, low = split(solved[k])
            right = turned[leaf, k * block : (k + 1) * block, :]
            total = total + (mul(high, right, NN) + mul(low, right, NN))
        skel_ref[leaf] = turned[leaf, red * block :, :]
        rows_ref[leaf] = total.astype(BF16)


def leaf_stage(near_blocks, leaf_basis, block):
    leaves, size = leaf_basis.shape[:2]
    red_size = size - block
    parts = size // block
    return pl.pallas_call(
        leaf_kernel,
        grid=(1,),
        in_specs=[
            pl.BlockSpec((leaves, 1, size, size), lambda g: (0, 0, 0, 0)),
            pl.BlockSpec((leaves, size, size), lambda g: (0, 0, 0)),
        ],
        out_specs=[
            pl.BlockSpec((leaves, red_size, red_size), lambda g: (0, 0, 0)),
            pl.BlockSpec((leaves, block, block), lambda g: (0, 0, 0)),
            pl.BlockSpec((leaves, block // 2 + SUB, block), lambda g: (0, 0, 0)),
            pl.BlockSpec((leaves, block, size), lambda g: (0, 0, 0)),
            pl.BlockSpec((leaves, block, size), lambda g: (0, 0, 0)),
        ],
        out_shape=[
            jax.ShapeDtypeStruct((leaves, red_size, red_size), F32),
            jax.ShapeDtypeStruct((leaves, block, block), F32),
            jax.ShapeDtypeStruct((leaves, block // 2 + SUB, block), F32),
            jax.ShapeDtypeStruct((leaves, block, size), BF16),
            jax.ShapeDtypeStruct((leaves, block, size), BF16),
        ],
        scratch_shapes=[
            pltpu.VMEM((leaves, parts, parts, block, block), F32),
            pltpu.VMEM((leaves, parts - 1, block, block), F32),
            pltpu.VMEM((leaves, size, size), BF16),
        ],
        compiler_params=pltpu.CompilerParams(vmem_limit_bytes=40 << 20),
        cost_estimate=pl.CostEstimate(
            flops=40_000_000_000, bytes_accessed=6_000_000, transcendentals=0
        ),
        name="leaf_stage",
    )(near_blocks, leaf_basis)


DEPTH = 4


def near_kernel(
    cols_ref, count_ref, place_ref, near_ref, own_ref, own_turned_ref, turned_ref, diag_ref, *rest
):
    devices = turned_ref.shape[0]
    skel_refs = rest[:devices]
    out_ref, skel, left_rows, buf, sems, skel_sems = rest[devices:]
    skel_copies = [
        pltpu.make_async_copy(skel_refs[d], skel.at[d], skel_sems.at[d]) for d in range(devices)
    ]
    leaves = own_ref.shape[0]
    block = diag_ref.shape[1]
    first = count_ref[0] - 1
    total = first
    for leaf in range(1, leaves):
        total = total + count_ref[leaf] - 1

    def place(w):
        leaf = jnp.int32(0)
        slot = w
        for other in range(leaves - 1):
            span = count_ref[other] - 1
            past = (leaf == other) & (slot >= span)
            slot = jnp.where(past, slot - span, slot)
            leaf = jnp.where(past, leaf + 1, leaf)
        return leaf, slot + 1

    def copy_of(w):
        leaf, slot = place(w)
        at = lax.rem(w, DEPTH)
        return pltpu.make_async_copy(near_ref.at[leaf, slot], buf.at[at], sems.at[at])

    for w in range(DEPTH - 1):

        @pl.when(w < total)
        def _(w=w):
            copy_of(jnp.int32(w)).start()

    for copy in skel_copies:
        copy.start()
    out_ref[...] = jnp.zeros_like(out_ref)
    for leaf in range(leaves):
        out_ref[leaf, 0] = diag_ref[leaf]
        left_rows[leaf, :block, :] = own_ref[leaf]
        left_rows[leaf, block:, :] = own_turned_ref[leaf]
    for copy in skel_copies:
        copy.wait()

    def body(w, _):
        @pl.when(w + DEPTH - 1 < total)
        def _():
            copy_of(w + DEPTH - 1).start()

        copy_of(w).wait()
        leaf, slot = place(w)
        other = cols_ref[leaf, slot] - place_ref[0]
        device = other // leaves
        inner = other - device * leaves
        distance = lax.rem(place_ref[1] - device + devices, devices)
        left = mul(left_rows[leaf], buf[lax.rem(w, DEPTH)], NN)
        skel_rows = left[:block]
        mixed = (skel_rows - left[block:]).astype(BF16)
        out_ref[leaf, slot] = mul(mixed, skel[distance, inner], NN) - mul(
            skel_rows.astype(BF16), turned_ref[device, inner], NT
        )
        return 0

    lax.fori_loop(0, total, body, 0)


def near_stage(near_blocks, near_cols, near_count, place, own_skel, own_turned, turned, diag, skels):
    leaves, slots = near_cols.shape
    size = near_blocks.shape[2]
    block = diag.shape[1]
    devices = len(skels)
    whole = pl.BlockSpec(memory_space=pltpu.VMEM)
    scalar = pl.BlockSpec(memory_space=pltpu.SMEM)
    left = pl.BlockSpec(memory_space=pl.ANY)
    return pl.pallas_call(
        near_kernel,
        in_specs=[scalar] * 3 + [left] + [whole] * 4 + [left] * devices,
        out_specs=whole,
        out_shape=jax.ShapeDtypeStruct((leaves, slots, block, block), F32),
        scratch_shapes=[
            pltpu.VMEM((devices, leaves, size, block), BF16),
            pltpu.VMEM((leaves, 2 * block, size), BF16),
            pltpu.VMEM((DEPTH, size, size), BF16),
            pltpu.SemaphoreType.DMA((DEPTH,)),
            pltpu.SemaphoreType.DMA((devices,)),
        ],
        compiler_params=pltpu.CompilerParams(vmem_limit_bytes=40 << 20),
        name="near_stage",
    )(near_cols, near_count, place, near_blocks, own_skel, own_turned, turned, diag, *skels)


def exchange_kernel(
    count, depth, schur_ref, turned_ref, schur_all, turned_all, own_sem, send_z, recv_z, send_x, recv_x
):
    width = count // depth
    me = lax.axis_index("col")
    z = me // width
    x = me % width
    away = sorted(range(1, depth), key=lambda d: min(d, depth - d))
    across = range(1, width)

    def along_z(d):
        return ((z + d) % depth) * width + x

    def along_x(e):
        return z * width + (x + e) % width

    barrier = pltpu.get_barrier_semaphore()
    for d in away:
        pl.semaphore_signal(barrier, inc=1, device_id={"col": along_z(d)})
    for e in across:
        pl.semaphore_signal(barrier, inc=1, device_id={"col": along_x(e)})
    pl.semaphore_wait(barrier, depth - 1 + width - 1)
    pairs = ((schur_ref, schur_all), (turned_ref, turned_all))
    started = []
    own = []
    for q, (source, target) in enumerate(pairs):
        for d in away:
            started.append(
                pltpu.make_async_remote_copy(
                    src_ref=source,
                    dst_ref=target.at[me],
                    send_sem=send_z.at[q, d],
                    recv_sem=recv_z.at[q, d],
                    device_id={"col": along_z(d)},
                )
            )
            started[-1].start()
        for e in across:
            started.append(
                pltpu.make_async_remote_copy(
                    src_ref=source,
                    dst_ref=target.at[me],
                    send_sem=send_x.at[q, 0, e],
                    recv_sem=recv_x.at[q, 0, e],
                    device_id={"col": along_x(e)},
                )
            )
            started[-1].start()
        own.append(pltpu.make_async_copy(source, target.at[me], own_sem.at[q]))
        own[-1].start()
    for q, (source, target) in enumerate(pairs):
        for d in away:
            block = along_z(depth - d)
            pltpu.make_async_remote_copy(
                src_ref=target.at[block],
                dst_ref=target.at[block],
                send_sem=send_z.at[q, d],
                recv_sem=recv_z.at[q, d],
                device_id={"col": block},
            ).wait_recv()
            for e in across:
                started.append(
                    pltpu.make_async_remote_copy(
                        src_ref=target.at[block],
                        dst_ref=target.at[block],
                        send_sem=send_x.at[q, d, e],
                        recv_sem=recv_x.at[q, d, e],
                        device_id={"col": along_x(e)},
                    )
                )
                started[-1].start()
    for q, (source, target) in enumerate(pairs):
        for d in [0] + away:
            for e in across:
                block = ((z + depth - d) % depth) * width + (x + width - e) % width
                pltpu.make_async_remote_copy(
                    src_ref=target.at[block],
                    dst_ref=target.at[block],
                    send_sem=send_x.at[q, d, e],
                    recv_sem=recv_x.at[q, d, e],
                    device_id={"col": along_x(width - e)},
                ).wait_recv()
    for copy in started:
        copy.wait_send()
    for copy in own:
        copy.wait()


def exchange(schur, turned, count):
    depth = 4 if count % 4 == 0 else count
    width = count // depth
    left = pl.BlockSpec(memory_space=pl.ANY)
    return pl.pallas_call(
        partial(exchange_kernel, count, depth),
        in_specs=[pl.BlockSpec(memory_space=pltpu.VMEM)] * 2,
        out_specs=[left] * 2,
        out_shape=[
            jax.ShapeDtypeStruct((count,) + schur.shape, schur.dtype),
            jax.ShapeDtypeStruct((count,) + turned.shape, turned.dtype),
        ],
        scratch_shapes=[
            pltpu.SemaphoreType.DMA((2,)),
            pltpu.SemaphoreType.DMA((2, depth)),
            pltpu.SemaphoreType.DMA((2, depth)),
            pltpu.SemaphoreType.DMA((2, depth, width)),
            pltpu.SemaphoreType.DMA((2, depth, width)),
        ],
        compiler_params=pltpu.CompilerParams(collective_id=0, has_side_effects=True),
        cost_estimate=pl.CostEstimate(flops=0, bytes_accessed=60_000_000, transcendentals=0),
        name="exchange",
    )(schur, turned)


def top_kernel(first_ref, second_ref, coupling_ref, basis_ref, factor_ref, schur_ref, merged, rotated):
    block = coupling_ref.shape[0]
    for at, ref in ((0, first_ref), (block, second_ref)):
        begin, corner, end = unpack(ref[...])
        merged[at : at + block, at : at + block] = jnp.concatenate(
            [
                jnp.concatenate([begin, corner.T], axis=1),
                jnp.concatenate([corner, end], axis=1),
            ],
            axis=0,
        )
    merged[:block, block:] = coupling_ref[...]
    merged[block:, :block] = coupling_ref[...].T
    basis = basis_ref[...]
    high, low = split(merged[...])
    high, low = split(mul(high, basis, NN) + mul(low, basis, NN))
    left = basis.T
    rotated[...] = mul(left, high, NN) + mul(left, low, NN)
    lowers, inverses = factor_blocks([rotated[:block, :block]])
    factor_ref[...] = lowers[0]
    tail = mul_three(rotated[block:, :block], inverses[0], NT)
    schur_ref[...] = rotated[block:, block:] - mul_three(tail, tail, NT)


def top_stage(first_block, second_block, coupling, basis):
    block = coupling.shape[0]
    whole = pl.BlockSpec(memory_space=pltpu.VMEM)
    return pl.pallas_call(
        top_kernel,
        in_specs=[whole] * 4,
        out_specs=[whole] * 2,
        out_shape=[jax.ShapeDtypeStruct((block, block), F32)] * 2,
        scratch_shapes=[
            pltpu.VMEM((2 * block, 2 * block), F32),
            pltpu.VMEM((2 * block, 2 * block), F32),
        ],
        cost_estimate=pl.CostEstimate(
            flops=10_000_000_000, bytes_accessed=600_000, transcendentals=0
        ),
        name="top_stage",
    )(first_block, second_block, coupling, basis)


def local(near_blocks, leaf_basis, near_cols, near_count, children, parent_basis, far_coupling):
    local_leaves = near_cols.shape[0]
    block = far_coupling.shape[1]
    red_size = leaf_basis.shape[1] - block
    row_index = lax.axis_index("row")
    col_index = lax.axis_index("col")
    col_count = lax.axis_size("col")
    row_count = lax.axis_size("row")
    group_size = local_leaves * col_count
    group_base = row_index * group_size
    skel = leaf_basis[:, :, red_size:]
    skels = [skel] + [
        lax.ppermute(skel, "col", [(c, (c + s) % col_count) for c in range(col_count)])
        for s in range(1, col_count)
    ]
    factors, diag_schur, packed, own_skel, own_turned = leaf_stage(near_blocks, leaf_basis, block)
    child_all, turned = exchange(packed, own_turned, col_count)
    child_all = child_all.reshape((group_size,) + packed.shape[1:])
    partner_row = row_index + 1 - 2 * (row_index % 2)
    parent_id = row_index * col_count + col_index
    first_block = child_all[children[parent_id, 0] - group_base]
    partner_parent = partner_row * col_count + col_index
    outgoing = child_all[children[partner_parent, 1] - group_base]
    route = [(r, r ^ 1) for r in range(row_count)]
    second_block = lax.ppermute(outgoing, "row", route)
    top_factor, top_schur = top_stage(first_block, second_block, far_coupling[0], parent_basis[0])
    place = jnp.stack([group_base, col_index]).astype(jnp.int32)
    near_schur = near_stage(
        near_blocks, near_cols, near_count, place, own_skel, own_turned, turned, diag_schur, skels
    )
    return (factors, near_schur, top_factor[None], top_schur[None])


def solution(mesh):
    placed = (
        P(("row", "col"), None, None, None),
        P(("row", "col"), None, None),
        P(("row", "col"), None),
        P(("row", "col")),
        P(),
        P(("row", "col"), None, None),
        P(("row", "col"), None, None),
    )
    return jax.shard_map(
        local,
        mesh=mesh,
        in_specs=placed,
        out_specs=(
            P(("row", "col"), None, None),
            P(("row", "col"), None, None, None),
            P(("row", "col"), None, None),
            P(("row", "col"), None, None),
        ),
        check_vma=False,
    )
```
